32 devices in a mesh: tgt: 4 (over z), ptr: 8 (over y, x, core).
Axes of the slice: x: 2, y: 2, z: 4, core: 2. Of those that a mesh axis runs over, the one named last changes fastest.
Arguments:
- targets: float32 [32, 32, 1024], P('tgt'), may hold values from -12 to 12
- partners: float32 [32, 32, 1024], P(None, None, 'ptr'), may hold values from -6 to 6
- occupied: int32 [8], P('ptr'), may hold values 0 or 1
- retained: int32 [1], replicated, may hold values from 16 to 32
Outputs:
- compressed: float32 [32, 32, 1024], P('tgt', 'ptr')
The draws below stay inside these ranges and needn't reach their ends.
All inputs are finite; a program needn't handle non-finite values. No bound on the sum of `occupied` on one device may be relied on, other than what follows from the above.
Results may differ from the reference program's by a relative error of at most 0.00008.
Values sent between devices are 32-bit elements; how exact they have to be, the bound alone decides.
A program may use at most 64 MiB of HBM per device.

```python
import math
import jax
import jax.numpy as jnp
from jax import lax

NG = 32
NT = 32
NP = 32
NBLK = 8


def draw_targets(key, part):
    key_base = jax.random.fold_in(key, 11)
    key_mixing = jax.random.fold_in(key, 12)
    key_planes = jax.random.fold_in(key, 13)
    fields = jax.random.normal(key_base, (NT, NG, NG * NG), jnp.float32)
    mixing = 0.09 * jax.random.normal(key_mixing, (NT, NT), jnp.float32)
    mixing = mixing + jnp.eye(NT, dtype=jnp.float32)
    rising = jnp.arange(NG).astype(jnp.float32) / (NG - 1)
    envelope = jnp.exp(rising * 1.0986123) * jax.random.uniform(key_planes, (NG,), jnp.float32, 0.7, 1.4)
    mixed = jnp.einsum('ab,bxm->axm', mixing, fields, precision=jax.lax.Precision.HIGHEST)
    return jnp.clip(mixed * envelope[None, :, None], -12.0, 12.0)


def place_ends(array, stream_key, low, top_value):
    longest = array.shape.index(max(array.shape))
    spots = []
    for shift in (0, 1):
        where = [jax.random.randint(jax.random.fold_in(stream_key, axis), (), 0, length) for axis, length in enumerate(array.shape)]
        where[longest] = (where[longest] + shift) % array.shape[longest]
        spots.append(tuple(where))
    return array.at[spots[0]].set(low).at[spots[1]].set(top_value)


def shard_levels(own_key, extent, split, low, largest):
    loudness = 1.0
    for position, shards_of in split:
        draws = jax.random.uniform(jax.random.fold_in(jax.random.fold_in(own_key, 6), position), (shards_of,), jnp.float32, low / len(split), largest / len(split))
        loudness = loudness * jnp.repeat(jnp.exp(draws), extent[position] // shards_of).reshape((-1,) + (1,) * (len(extent) - 1 - position))
    return loudness


def scatter_about(stream_key, extent, width, reach, cuts=(), held_as=jnp.bfloat16):
    factor_of = shard_levels(stream_key, extent, cuts, -0.22, 0.18) if cuts else 1.0
    drawn = jax.random.normal(stream_key, extent, jnp.float32) * width * factor_of
    return jnp.minimum(jnp.maximum(drawn, -reach), reach).astype(held_as)


def setup_inputs(seed: int = 0) -> dict:
    seeds = jax.random.split(jax.random.key(seed), 5)
    return {
        "targets": draw_targets(jax.random.fold_in(seeds[4], 71), 0),
        "partners": scatter_about(seeds[1], (NG, NG, NP * NG), 1.0, 6.0, ((2, 8),), jnp.float32),
        "occupied": place_ends((jax.random.randint(seeds[2], (NBLK,), 0, 4) < 3).astype(jnp.int32), jax.random.fold_in(seeds[2], 1), 0, 1),
        "retained": jax.random.randint(seeds[3], (1,), NT // 2, NT + 1).astype(jnp.int32),
    }


def coulomb_table(length):
    indices = jnp.arange(length, dtype=jnp.int32)
    signed = jnp.where(indices < length // 2, indices, indices - length).astype(jnp.float32)
    wave = signed * (2.0 * math.pi / length)
    wave = wave * wave
    total = wave[:, None, None] + wave[None, :, None] + wave[None, None, :]
    safe = jnp.where(total > 0.0, total, jnp.float32(1.0))
    return jnp.where(total > 0.0, 4.0 * math.pi / safe, jnp.float32(0.0))

def reference(targets, partners, occupied, retained):
    ncells = NG * NG * NG
    coulomb = coulomb_table(NG)
    orbitals = jnp.transpose(partners.reshape(NG, NG, NP, NG), (2, 0, 1, 3))
    occupancy = 0.25 + 0.75 * jnp.repeat(occupied.astype(jnp.float32), 4)
    weighted = orbitals * occupancy[:, None, None, None]

    def action(target_one):
        density = target_one.reshape(NG, NG, NG)[None] * orbitals
        spectrum = jnp.fft.fftn(density, axes=(1, 2, 3))
        potential = jnp.real(jnp.fft.ifftn(spectrum * coulomb[None], axes=(1, 2, 3)))
        return jnp.sum(weighted * potential, axis=0).reshape(NG, NG * NG)
    actions = lax.map(action, targets)
    intersection = jnp.einsum('axm,bxm->ab', targets, actions, precision=lax.Precision.HIGHEST) / ncells
    lower = jnp.linalg.cholesky(intersection)
    inverse = jax.scipy.linalg.solve_triangular(lower, jnp.eye(NT, dtype=jnp.float32), lower=True)
    result = jnp.einsum('bc,cxm->bxm', inverse, actions, precision=lax.Precision.HIGHEST)
    keeping = (jnp.arange(NT, dtype=jnp.int32) < retained[0]).astype(jnp.float32)
    return result * keeping[:, None, None]
```

```python
import functools
import math

import jax
import jax.numpy as jnp
import numpy as np
from jax import lax
from jax.experimental import pallas as pl
from jax.experimental.pallas import tpu as pltpu
from jax.sharding import PartitionSpec as P

HIGHEST = lax.Precision.HIGHEST
MESH = pl.DeviceIdType.MESH


def real_dft(values):
    n = len(values)
    if n == 1:
        return [values[0]], [None]
    even_re, even_im = real_dft(values[0::2])
    odd_re, odd_im = real_dft(values[1::2])
    half = n // 2
    re, im = [None] * (half + 1), [None] * (half + 1)
    re[0], re[half] = even_re[0] + odd_re[0], even_re[0] - odd_re[0]
    for k in range(1, half // 2 + 1):
        if 2 * k == half:
            re[k], im[k] = even_re[k], -odd_re[k]
            continue
        c, s = math.cos(2 * math.pi * k / n), -math.sin(2 * math.pi * k / n)
        if 8 * k == n:
            a = c * (odd_re[k] + odd_im[k]) if odd_im[k] is not None else c * odd_re[k]
            b = c * (odd_im[k] - odd_re[k]) if odd_im[k] is not None else -c * odd_re[k]
        else:
            a = c * odd_re[k] - s * odd_im[k]
            b = s * odd_re[k] + c * odd_im[k]
        re[k], re[half - k] = even_re[k] + a, even_re[k] - a
        im[k], im[half - k] = even_im[k] + b, b - even_im[k]
    return re, im


def real_dft_transposed(re, im):
    half = len(re) - 1
    if half == 0:
        return [re[0]]
    n = 2 * half
    quarter = half // 2
    even_re, even_im = [None] * (quarter + 1), [None] * (quarter + 1)
    odd_re, odd_im = [None] * (quarter + 1), [None] * (quarter + 1)
    even_re[0], odd_re[0] = re[0] + re[half], re[0] - re[half]
    for k in range(1, quarter + 1):
        if 2 * k == half:
            even_re[k], odd_re[k] = re[k], -im[k]
            continue
        c, s = math.cos(2 * math.pi * k / n), -math.sin(2 * math.pi * k / n)
        even_re[k], even_im[k] = re[k] + re[half - k], im[k] - im[half - k]
        a, b = re[k] - re[half - k], im[k] + im[half - k]
        if 8 * k == n:
            odd_re[k], odd_im[k] = c * (a - b), c * (a + b)
        else:
            odd_re[k], odd_im[k] = c * a + s * b, c * b - s * a
    values = [None] * n
    values[0::2] = real_dft_transposed(even_re[: quarter + 1], even_im[: quarter + 1])
    values[1::2] = real_dft_transposed(odd_re[: quarter + 1], odd_im[: quarter + 1])
    return values


def flat_dft(values):
    re, im = real_dft(values)
    return re + im[1:-1]


def flat_dft_transposed(modes):
    half = len(modes) // 2
    return real_dft_transposed(modes[: half + 1], [None] + modes[half + 1 :] + [None])


def split_product(field, weights):
    width = field.shape[1]
    high = field.astype(jnp.bfloat16)
    low = (field - high.astype(jnp.float32)).astype(jnp.bfloat16)
    both = jnp.dot(
        jnp.concatenate([high, low], axis=1), weights, preferred_element_type=jnp.float32
    )
    return both[:, :width] + both[:, width:]


def action_kernel(t_ref, psi_ref, occ_ref, weights_ref, table_ref, out_ref, spec):
    length, rows, cells = t_ref.shape
    lanes = psi_ref.shape[2]
    groups = lanes // length
    group_of = lax.broadcasted_iota(jnp.int32, (rows, lanes), 1) // length
    at_group = [group_of == g for g in range(groups)]

    def pick(options):
        chosen = options[0]
        for g in range(1, groups):
            chosen = jnp.where(at_group[g], options[g], chosen)
        return chosen

    def rolled(value, steps):
        steps = steps % groups
        return value if steps == 0 else pltpu.roll(value, steps * length, 1)

    @pl.loop(0, length)
    def forward(x):
        density = []
        for q in range(length // groups):
            v = t_ref[x, :, q * lanes : (q + 1) * lanes]
            turned = [rolled(v, s) for s in range(groups)]
            for g in range(groups):
                y = q * groups + g
                spread = pick([turned[(h - g) % groups] for h in range(groups)])
                density.append(spread * psi_ref[x, y : y + 1, :])
        waves = split_product(jnp.concatenate(density, axis=0), weights_ref[...])
        modes = flat_dft([waves[y * rows : (y + 1) * rows] for y in range(length)])
        for m in range(length):
            spec[x, m] = modes[m]

    @pl.loop(0, length)
    def middle(m):
        modes = flat_dft([spec[x, m] for x in range(length)])
        half = length // 2
        scaled = []
        for i in range(length):
            k = i if i <= half else i - half
            scaled.append(modes[i] * table_ref[m, k : k + 1, :])
        values = flat_dft_transposed(scaled)
        for x in range(length):
            spec[x, m] = values[x]

    @pl.loop(0, length)
    def backward(x):
        values = flat_dft_transposed([spec[x, m] for m in range(length)])
        potential = split_product(jnp.concatenate(values, axis=0), weights_ref[...])
        occ = occ_ref[0:1, :]
        for q in range(length // groups):
            terms = []
            for g in range(groups):
                y = q * groups + g
                terms.append(
                    potential[y * rows : (y + 1) * rows] * (psi_ref[x, y : y + 1, :] * occ)
                )
            total = None
            for s in range(groups):
                part = rolled(pick([terms[(h - s) % groups] for h in range(groups)]), -s)
                total = part if total is None else total + part
            out_ref[x, :, q * lanes : (q + 1) * lanes] = total


def join_kernel(
    tn, pn, part_ref, t_ref, out_ref, rs_buf, t_buf, a_buf, g_buf, inv_ref,
    rs_send, rs_recv, t_send, t_recv, a_send, a_recv, g_send, g_recv,
):
    t, p = lax.axis_index("tgt"), lax.axis_index("ptr")
    slab = part_ref.shape[0] // pn
    rows = part_ref.shape[1]
    cells = part_ref.shape[2]
    all_cells = part_ref.shape[0] * cells
    total_rows = tn * rows
    width = inv_ref.shape[1]

    barrier = pltpu.get_barrier_semaphore()

    @pl.loop(1, tn * pn)
    def greet(d):
        other = lax.rem(t * pn + p + d, tn * pn)
        pl.semaphore_signal(
            barrier, inc=1, device_id=(other // pn, lax.rem(other, pn)), device_id_type=MESH
        )

    pl.semaphore_wait(barrier, tn * pn - 1)

    def rs_copy(q, slot):
        return pltpu.make_async_remote_copy(
            src_ref=part_ref.at[pl.ds(q * slab, slab)], dst_ref=rs_buf.at[slot],
            send_sem=rs_send.at[q], recv_sem=rs_recv.at[slot],
            device_id=(t, q), device_id_type=MESH,
        )

    def t_copy(s, slot):
        return pltpu.make_async_remote_copy(
            src_ref=t_ref.at[pl.ds(p * slab, slab)], dst_ref=t_buf.at[slot],
            send_sem=t_send.at[s], recv_sem=t_recv.at[slot],
            device_id=(s, p), device_id_type=MESH,
        )

    def a_copy(s, slot):
        return pltpu.make_async_remote_copy(
            src_ref=a_buf.at[t], dst_ref=a_buf.at[slot],
            send_sem=a_send.at[s], recv_sem=a_recv.at[slot],
            device_id=(s, p), device_id_type=MESH,
        )

    def g_copy(other, slot):
        return pltpu.make_async_remote_copy(
            src_ref=g_buf.at[t * pn + p], dst_ref=g_buf.at[slot],
            send_sem=g_send.at[other], recv_sem=g_recv.at[slot],
            device_id=(other // pn, lax.rem(other, pn)), device_id_type=MESH,
        )

    for d in range(1, pn):
        rs_copy(lax.rem(p + d, pn), p).start()
    for d in range(1, tn):
        t_copy(lax.rem(t + d, tn), t).start()
    t_buf[t] = t_ref[pl.ds(p * slab, slab)]
    own = part_ref[pl.ds(p * slab, slab)]
    for d in range(1, pn):
        q = lax.rem(p + d, pn)
        rs_copy(q, q).wait_recv()
        own = own + rs_buf[q]
    a_buf[t] = own
    for d in range(1, tn):
        a_copy(lax.rem(t + d, tn), t).start()
    for d in range(1, tn):
        s = lax.rem(t + d, tn)
        t_copy(s, s).wait_recv()
    gram = jnp.zeros((rows, total_rows), jnp.float32)
    for x in range(slab):
        every = jnp.concatenate([t_buf[s, x] for s in range(tn)], axis=0)
        gram = gram + lax.dot_general(
            own[x], every, (((1,), (1,)), ((), ())),
            precision=HIGHEST, preferred_element_type=jnp.float32,
        )
    gram = gram * (1.0 / all_cells)
    g_buf[t * pn + p] = jnp.concatenate(
        [gram, jnp.zeros((rows, width - total_rows), jnp.float32)], axis=1
    )

    @pl.loop(1, tn * pn)
    def spread(d):
        g_copy(lax.rem(t * pn + p + d, tn * pn), t * pn + p).start()

    @pl.loop(1, tn * pn)
    def collect(d):
        other = lax.rem(t * pn + p + d, tn * pn)
        g_copy(other, other).wait_recv()

    blocks = []
    for s in range(tn):
        block = g_buf[s * pn]
        for q in range(1, pn):
            block = block + g_buf[s * pn + q]
        blocks.append(block)
    square = jnp.concatenate(blocks, axis=0)
    padded = jnp.concatenate([square, jnp.zeros((width - total_rows, width), jnp.float32)], axis=0)
    symmetric = 0.5 * (square + jnp.transpose(padded)[:total_rows])
    row_of = lax.broadcasted_iota(jnp.int32, (total_rows, width), 0)
    lane_of = lax.broadcasted_iota(jnp.int32, (total_rows, width), 1)
    work = jnp.where(lane_of == row_of + total_rows, 1.0, symmetric)
    for k in range(total_rows - 1):
        row = work[k : k + 1, :]
        scaled = row / work[k : k + 1, k : k + 1]
        column = jnp.where(row_of > k, work[:, k : k + 1], 0.0)
        work = work - column * scaled
    pivots = jnp.sum(jnp.where(lane_of == row_of, work, 0.0), axis=1, keepdims=True)
    inv_ref[...] = work * (1.0 / jnp.sqrt(pivots))
    mine = inv_ref[pl.ds(pl.multiple_of(t * rows, rows), rows), :][:, total_rows : 2 * total_rows]
    for d in range(1, tn):
        s = lax.rem(t + d, tn)
        a_copy(s, s).wait_recv()
    for x in range(slab):
        every = jnp.concatenate([a_buf[s, x] for s in range(tn)], axis=0)
        out_ref[x] = jnp.dot(mine, every, precision=HIGHEST, preferred_element_type=jnp.float32)

    for d in range(1, pn):
        rs_copy(lax.rem(p + d, pn), p).wait_send()
    for d in range(1, tn):
        t_copy(lax.rem(t + d, tn), t).wait_send()
        a_copy(lax.rem(t + d, tn), t).wait_send()

    @pl.loop(1, tn * pn)
    def drain(d):
        g_copy(lax.rem(t * pn + p + d, tn * pn), t * pn + p).wait_send()


def constants(length, groups):
    i = np.arange(length)
    phase = 2.0 * np.pi / length * (i[:, None] * i[None, :] % length)
    cas = np.kron(np.eye(groups), np.cos(phase) + np.sin(phase)).astype(np.float32)
    high = cas.astype(jnp.bfloat16)
    low = (cas - high.astype(np.float32)).astype(jnp.bfloat16)
    weights = np.concatenate([np.concatenate([high, low], 1)] * 2, 0)
    signed = np.where(i < length // 2, i, i - length)
    half = length // 2
    k = np.arange(half + 1)
    wave = (2.0 * np.pi / length) ** 2
    total = wave * ((k**2)[:, None, None] + (k**2)[None, :, None] + (signed**2)[None, None, :])
    coulomb = np.where(total > 0, 4 * np.pi / np.where(total > 0, total, 1.0), 0.0)
    fold = np.where((k == 0) | (k == half), 1.0, 2.0)
    coulomb = coulomb * fold[:, None, None] * fold[None, :, None] / length**3
    order = np.concatenate([np.arange(half + 1), np.arange(1, half)])
    table = np.tile(coulomb[order], (1, 1, groups)).astype(np.float32)
    return weights, table


def shards(tn, pn, targets, partners, occupied, retained):
    rows, length, cells = targets.shape
    lanes = partners.shape[2]
    groups = lanes // length
    slab = length // pn
    weights, table = constants(length, groups)
    per_block = groups // occupied.shape[0]
    occupancy = 0.25 + 0.75 * jnp.repeat(occupied.astype(jnp.float32), per_block * length)
    planes = jnp.transpose(targets, (1, 0, 2))
    vmem = pl.BlockSpec(memory_space=pltpu.VMEM)
    partial = pl.pallas_call(
        action_kernel,
        out_shape=jax.ShapeDtypeStruct((length, rows, cells), jnp.float32),
        in_specs=[vmem] * 5,
        out_specs=vmem,
        scratch_shapes=[pltpu.VMEM((length, length, rows, lanes), jnp.float32)],
        name="actions",
    )(planes, partners, occupancy[None, :], jnp.asarray(weights), jnp.asarray(table))
    total_rows = tn * rows
    width = -(-2 * total_rows // 128) * 128
    dma = pltpu.SemaphoreType.DMA
    block = pltpu.VMEM((tn, slab, rows, cells), jnp.float32)
    result = pl.pallas_call(
        functools.partial(join_kernel, tn, pn),
        out_shape=jax.ShapeDtypeStruct((slab, rows, cells), jnp.float32),
        in_specs=[vmem] * 2,
        out_specs=vmem,
        scratch_shapes=[
            pltpu.VMEM((pn, slab, rows, cells), jnp.float32),
            block,
            block,
            pltpu.VMEM((tn * pn, rows, width), jnp.float32),
            pltpu.VMEM((total_rows, width), jnp.float32),
            dma((pn,)), dma((pn,)), dma((tn,)), dma((tn,)),
            dma((tn,)), dma((tn,)), dma((tn * pn,)), dma((tn * pn,)),
        ],
        compiler_params=pltpu.CompilerParams(collective_id=0, has_side_effects=True),
        name="join",
    )(partial, planes)
    global_rows = lax.axis_index("tgt") * rows + jnp.arange(rows, dtype=jnp.int32)
    keeping = (global_rows < retained[0]).astype(jnp.float32)
    return jnp.transpose(result, (1, 0, 2)) * keeping[:, None, None]


def solution(mesh):
    return jax.shard_map(
        functools.partial(shards, mesh.shape["tgt"], mesh.shape["ptr"]),
        mesh=mesh,
        in_specs=(P("tgt", None, None), P(None, None, "ptr"), P("ptr"), P()),
        out_specs=P("tgt", "ptr", None),
        check_vma=False,
    )
```

```python
import functools
import math

import jax
import jax.numpy as jnp
import numpy as np
from jax import lax
from jax.experimental import pallas as pl
from jax.experimental.pallas import tpu as pltpu
from jax.sharding import PartitionSpec as P

HIGHEST = lax.Precision.HIGHEST
MESH = pl.DeviceIdType.MESH
FORWARD = 4
BACKWARD = 4


def real_dft(values):
    n = len(values)
    if n == 1:
        return [values[0]], [None]
    even_re, even_im = real_dft(values[0::2])
    odd_re, odd_im = real_dft(values[1::2])
    half = n // 2
    re, im = [None] * (half + 1), [None] * (half + 1)
    re[0], re[half] = even_re[0] + odd_re[0], even_re[0] - odd_re[0]
    for k in range(1, half // 2 + 1):
        if 2 * k == half:
            re[k], im[k] = even_re[k], -odd_re[k]
            continue
        c, s = math.cos(2 * math.pi * k / n), -math.sin(2 * math.pi * k / n)
        if 8 * k == n:
            a = c * (odd_re[k] + odd_im[k]) if odd_im[k] is not None else c * odd_re[k]
            b = c * (odd_im[k] - odd_re[k]) if odd_im[k] is not None else -c * odd_re[k]
        else:
            a = c * odd_re[k] - s * odd_im[k]
            b = s * odd_re[k] + c * odd_im[k]
        re[k], re[half - k] = even_re[k] + a, even_re[k] - a
        im[k], im[half - k] = even_im[k] + b, b - even_im[k]
    return re, im


def real_dft_transposed(re, im):
    half = len(re) - 1
    if half == 0:
        return [re[0]]
    n = 2 * half
    quarter = half // 2
    even_re, even_im = [None] * (quarter + 1), [None] * (quarter + 1)
    odd_re, odd_im = [None] * (quarter + 1), [None] * (quarter + 1)
    even_re[0], odd_re[0] = re[0] + re[half], re[0] - re[half]
    for k in range(1, quarter + 1):
        if 2 * k == half:
            even_re[k], odd_re[k] = re[k], -im[k]
            continue
        c, s = math.cos(2 * math.pi * k / n), -math.sin(2 * math.pi * k / n)
        even_re[k], even_im[k] = re[k] + re[half - k], im[k] - im[half - k]
        a, b = re[k] - re[half - k], im[k] + im[half - k]
        if 8 * k == n:
            odd_re[k], odd_im[k] = c * (a - b), c * (a + b)
        else:
            odd_re[k], odd_im[k] = c * a + s * b, c * b - s * a
    values = [None] * n
    values[0::2] = real_dft_transposed(even_re[: quarter + 1], even_im[: quarter + 1])
    values[1::2] = real_dft_transposed(odd_re[: quarter + 1], odd_im[: quarter + 1])
    return values


def flat_dft(values):
    re, im = real_dft(values)
    return re + im[1:-1]


def flat_dft_transposed(modes):
    half = len(modes) // 2
    return real_dft_transposed(modes[: half + 1], [None] + modes[half + 1 :] + [None])


def split_product(field, weights):
    width = field.shape[1]
    high = field.astype(jnp.bfloat16)
    low = (field - high.astype(jnp.float32)).astype(jnp.bfloat16)
    both = jnp.dot(
        jnp.concatenate([high, low], axis=1), weights, preferred_element_type=jnp.float32
    )
    return both[:, :width] + both[:, width:]


def kernel(
    tn, pn, t_hbm, psi_ref, weights_ref, table_ref, occupied_ref, retained_ref, out_ref,
    planes, spec, part, rs_buf, t_buf, a_buf, gram_ref, g_buf, inv_ref,
    load_sem, rs_send, rs_recv, t_send, t_recv, a_send, a_recv, g_send, g_recv,
):
    t, p = lax.axis_index("tgt"), lax.axis_index("ptr")
    length, rows, cells = planes.shape
    lanes = psi_ref.shape[2]
    groups = lanes // length
    slab = length // pn
    all_cells = length * cells
    total_rows = tn * rows
    width = inv_ref.shape[1]
    me = t * pn + p
    devices = tn * pn

    loads = [
        pltpu.make_async_copy(t_hbm.at[a], planes.at[:, a, :], load_sem.at[a]) for a in range(rows)
    ]
    for load in loads:
        load.start()

    barrier = pltpu.get_barrier_semaphore()

    @pl.loop(1, devices)
    def greet(d):
        other = lax.rem(me + d, devices)
        pl.semaphore_signal(
            barrier, inc=1, device_id=(other // pn, lax.rem(other, pn)), device_id_type=MESH
        )

    pl.semaphore_wait(barrier, devices - 1)
    for load in loads:
        load.wait()

    def rs_copy(q, slot, r):
        return pltpu.make_async_remote_copy(
            src_ref=part.at[q * slab + r], dst_ref=rs_buf.at[slot, r],
            send_sem=rs_send.at[q, r], recv_sem=rs_recv.at[slot, r],
            device_id=(t, q), device_id_type=MESH,
        )

    def t_copy(s, slot):
        return pltpu.make_async_remote_copy(
            src_ref=planes.at[pl.ds(p * slab, slab)], dst_ref=t_buf.at[slot],
            send_sem=t_send.at[s], recv_sem=t_recv.at[slot],
            device_id=(s, p), device_id_type=MESH,
        )

    def a_copy(s, slot, r):
        return pltpu.make_async_remote_copy(
            src_ref=a_buf.at[t, r], dst_ref=a_buf.at[slot, r],
            send_sem=a_send.at[s, r], recv_sem=a_recv.at[slot, r],
            device_id=(s, p), device_id_type=MESH,
        )

    def g_copy(other, slot):
        return pltpu.make_async_remote_copy(
            src_ref=g_buf.at[me], dst_ref=g_buf.at[slot],
            send_sem=g_send.at[other], recv_sem=g_recv.at[slot],
            device_id=(other // pn, lax.rem(other, pn)), device_id_type=MESH,
        )

    for d in range(1, tn):
        t_copy(lax.rem(t + d, tn), t).start()

    group_of = lax.broadcasted_iota(jnp.int32, (rows, lanes), 1) // length
    at_group = [group_of == g for g in range(groups)]
    per_block = groups // occupied_ref.shape[0]
    occ = 0.25 + 0.75 * occupied_ref[0].astype(jnp.float32) * jnp.ones((rows, lanes), jnp.float32)
    for i in range(1, occupied_ref.shape[0]):
        level = 0.25 + 0.75 * occupied_ref[i].astype(jnp.float32)
        occ = jnp.where(group_of >= i * per_block, level, occ)

    def pick(options):
        chosen = options[0]
        for g in range(1, groups):
            chosen = jnp.where(at_group[g], options[g], chosen)
        return chosen

    def rolled(value, steps):
        steps = steps % groups
        return value if steps == 0 else pltpu.roll(value, steps * length, 1)

    plane_rows = length * rows

    @pl.loop(0, length // FORWARD)
    def forward(i):
        density = []
        for j in range(FORWARD):
            x = i * FORWARD + j
            for q in range(length // groups):
                v = planes[x, :, q * lanes : (q + 1) * lanes]
                turned = [rolled(v, s) for s in range(groups)]
                for g in range(groups):
                    y = q * groups + g
                    spread = pick([turned[(h - g) % groups] for h in range(groups)])
                    density.append(spread * psi_ref[x, y : y + 1, :])
        waves = split_product(jnp.concatenate(density, axis=0), weights_ref[...])
        for j in range(FORWARD):
            wave = waves[j * plane_rows : (j + 1) * plane_rows]
            modes = flat_dft([wave[y * rows : (y + 1) * rows] for y in range(length)])
            for m in range(length):
                spec[i * FORWARD + j, m] = modes[m]

    @pl.loop(0, length)
    def middle(m):
        modes = flat_dft([spec[x, m] for x in range(length)])
        half = length // 2
        scaled = []
        for i in range(length):
            k = i if i <= half else i - half
            scaled.append(modes[i] * table_ref[m, k : k + 1, :])
        values = flat_dft_transposed(scaled)
        for x in range(length):
            spec[x, m] = values[x]

    gram_ref[...] = jnp.zeros_like(gram_ref)

    def reduce_round(r):
        own = part[p * slab + r]
        for d in range(1, pn):
            q = lax.rem(p + d, pn)
            rs_copy(q, q, r).wait_recv()
            own = own + rs_buf[q, r]
        a_buf[t, r] = own
        for d in range(1, tn):
            a_copy(lax.rem(t + d, tn), t, r).start()
        every = jnp.concatenate([t_buf[s, r] for s in range(tn)], axis=0)
        gram_ref[...] += lax.dot_general(
            own, every, (((1,), (1,)), ((), ())),
            precision=HIGHEST, preferred_element_type=jnp.float32,
        )

    @pl.loop(0, slab)
    def rounds(r):
        @pl.loop(0, pn // BACKWARD)
        def backward(i):
            owners = [lax.rem(p + 1 + i * BACKWARD + j, pn) for j in range(BACKWARD)]
            values = []
            for q in owners:
                values += flat_dft_transposed([spec[q * slab + r, m] for m in range(length)])
            potentials = split_product(jnp.concatenate(values, axis=0), weights_ref[...])
            for j, owner in enumerate(owners):
                x = owner * slab + r
                potential = potentials[j * plane_rows : (j + 1) * plane_rows]
                for q in range(length // groups):
                    terms = []
                    for g in range(groups):
                        y = q * groups + g
                        terms.append(potential[y * rows : (y + 1) * rows] * psi_ref[x, y : y + 1, :])
                    total = None
                    for s in range(groups):
                        chosen = pick([terms[(h - s) % groups] for h in range(groups)])
                        moved = rolled(chosen * occ, -s)
                        total = moved if total is None else total + moved
                    part[x, :, q * lanes : (q + 1) * lanes] = total
            for j in range(BACKWARD):
                @pl.when(i * BACKWARD + j < pn - 1)
                def send():
                    rs_copy(owners[j], p, r).start()

        @pl.when(r == 0)
        def targets_in():
            t_buf[t] = planes[pl.ds(p * slab, slab)]
            for d in range(1, tn):
                s = lax.rem(t + d, tn)
                t_copy(s, s).wait_recv()

        @pl.when(r > 0)
        def earlier():
            reduce_round(r - 1)

    reduce_round(slab - 1)

    gram = gram_ref[...] * (1.0 / all_cells)
    g_buf[me] = jnp.concatenate(
        [gram, jnp.zeros((rows, width - total_rows), jnp.float32)], axis=1
    )

    @pl.loop(1, devices)
    def spread_gram(d):
        g_copy(lax.rem(me + d, devices), me).start()

    @pl.loop(1, devices)
    def collect(d):
        other = lax.rem(me + d, devices)
        g_copy(other, other).wait_recv()

    blocks = []
    for s in range(tn):
        block = g_buf[s * pn]
        for q in range(1, pn):
            block = block + g_buf[s * pn + q]
        blocks.append(block)
    square = jnp.concatenate(blocks, axis=0)
    padded = jnp.concatenate([square, jnp.zeros((width - total_rows, width), jnp.float32)], axis=0)
    symmetric = 0.5 * (square + jnp.transpose(padded)[:total_rows])
    row_of = lax.broadcasted_iota(jnp.int32, (total_rows, width), 0)
    lane_of = lax.broadcasted_iota(jnp.int32, (total_rows, width), 1)
    work = jnp.where(lane_of == row_of + total_rows, 1.0, symmetric)
    for k in range(total_rows - 1):
        row = work[k : k + 1, :]
        scaled = row / work[k : k + 1, k : k + 1]
        column = jnp.where(row_of > k, work[:, k : k + 1], 0.0)
        work = work - column * scaled
    pivots = jnp.sum(jnp.where(lane_of == row_of, work, 0.0), axis=1, keepdims=True)
    keeping = (row_of < retained_ref[0]).astype(jnp.float32)
    inv_ref[...] = work * (1.0 / jnp.sqrt(pivots)) * keeping
    mine = inv_ref[pl.ds(pl.multiple_of(t * rows, rows), rows), :][:, total_rows : 2 * total_rows]
    for d in range(1, tn):
        s = lax.rem(t + d, tn)
        for r in range(slab):
            a_copy(s, s, r).wait_recv()
    for x in range(slab):
        every = jnp.concatenate([a_buf[s, x] for s in range(tn)], axis=0)
        out_ref[:, x, :] = jnp.dot(
            mine, every, precision=HIGHEST, preferred_element_type=jnp.float32
        )

    for d in range(1, pn):
        for r in range(slab):
            rs_copy(lax.rem(p + d, pn), p, r).wait_send()
    for d in range(1, tn):
        t_copy(lax.rem(t + d, tn), t).wait_send()
        for r in range(slab):
            a_copy(lax.rem(t + d, tn), t, r).wait_send()

    @pl.loop(1, devices)
    def drain(d):
        g_copy(lax.rem(me + d, devices), me).wait_send()


def constants(length, groups):
    i = np.arange(length)
    phase = 2.0 * np.pi / length * (i[:, None] * i[None, :] % length)
    cas = np.kron(np.eye(groups), np.cos(phase) + np.sin(phase)).astype(np.float32)
    high = cas.astype(jnp.bfloat16)
    low = (cas - high.astype(np.float32)).astype(jnp.bfloat16)
    weights = np.concatenate([np.concatenate([high, low], 1)] * 2, 0)
    signed = np.where(i < length // 2, i, i - length)
    half = length // 2
    k = np.arange(half + 1)
    wave = (2.0 * np.pi / length) ** 2
    total = wave * ((k**2)[:, None, None] + (k**2)[None, :, None] + (signed**2)[None, None, :])
    coulomb = np.where(total > 0, 4 * np.pi / np.where(total > 0, total, 1.0), 0.0)
    fold = np.where((k == 0) | (k == half), 1.0, 2.0)
    coulomb = coulomb * fold[:, None, None] * fold[None, :, None] / length**3
    order = np.concatenate([np.arange(half + 1), np.arange(1, half)])
    table = np.tile(coulomb[order], (1, 1, groups)).astype(np.float32)
    return weights, table


def shards(tn, pn, targets, partners, occupied, retained):
    rows, length, cells = targets.shape
    lanes = partners.shape[2]
    groups = lanes // length
    slab = length // pn
    weights, table = constants(length, groups)
    total_rows = tn * rows
    width = -(-2 * total_rows // 128) * 128
    vmem = pl.BlockSpec(memory_space=pltpu.VMEM)
    smem = pl.BlockSpec(memory_space=pltpu.SMEM)
    dma = pltpu.SemaphoreType.DMA
    planes = pltpu.VMEM((length, rows, cells), jnp.float32)
    block = pltpu.VMEM((tn, slab, rows, cells), jnp.float32)
    return pl.pallas_call(
        functools.partial(kernel, tn, pn),
        out_shape=jax.ShapeDtypeStruct((rows, slab, cells), jnp.float32),
        in_specs=[pl.BlockSpec(memory_space=pl.ANY), vmem, vmem, vmem, smem, smem],
        out_specs=vmem,
        scratch_shapes=[
            planes,
            pltpu.VMEM((length, length, rows, lanes), jnp.float32),
            planes,
            pltpu.VMEM((pn, slab, rows, cells), jnp.float32),
            block,
            block,
            pltpu.VMEM((rows, total_rows), jnp.float32),
            pltpu.VMEM((tn * pn, rows, width), jnp.float32),
            pltpu.VMEM((total_rows, width), jnp.float32),
            dma((rows,)), dma((pn, slab)), dma((pn, slab)), dma((tn,)), dma((tn,)),
            dma((tn, slab)), dma((tn, slab)), dma((tn * pn,)), dma((tn * pn,)),
        ],
        compiler_params=pltpu.CompilerParams(collective_id=0, has_side_effects=True),
        name="exchange",
    )(targets, partners, jnp.asarray(weights), jnp.asarray(table), occupied, retained)


def solution(mesh):
    return jax.shard_map(
        functools.partial(shards, mesh.shape["tgt"], mesh.shape["ptr"]),
        mesh=mesh,
        in_specs=(P("tgt", None, None), P(None, None, "ptr"), P("ptr"), P()),
        out_specs=P("tgt", "ptr", None),
        check_vma=False,
    )
```

```python
import functools
import math

import jax
import jax.numpy as jnp
import numpy as np
from jax import lax
from jax.experimental import pallas as pl
from jax.experimental.pallas import tpu as pltpu
from jax.sharding import PartitionSpec as P

HIGHEST = lax.Precision.HIGHEST
MESH = pl.DeviceIdType.MESH
FORWARD = 4
BACKWARD = 4


def real_dft(values):
    n = len(values)
    if n == 1:
        return [values[0]], [None]
    even_re, even_im = real_dft(values[0::2])
    odd_re, odd_im = real_dft(values[1::2])
    half = n // 2
    re, im = [None] * (half + 1), [None] * (half + 1)
    re[0], re[half] = even_re[0] + odd_re[0], even_re[0] - odd_re[0]
    for k in range(1, half // 2 + 1):
        if 2 * k == half:
            re[k], im[k] = even_re[k], -odd_re[k]
            continue
        c, s = math.cos(2 * math.pi * k / n), -math.sin(2 * math.pi * k / n)
        if 8 * k == n:
            a = c * (odd_re[k] + odd_im[k]) if odd_im[k] is not None else c * odd_re[k]
            b = c * (odd_im[k] - odd_re[k]) if odd_im[k] is not None else -c * odd_re[k]
        else:
            a = c * odd_re[k] - s * odd_im[k]
            b = s * odd_re[k] + c * odd_im[k]
        re[k], re[half - k] = even_re[k] + a, even_re[k] - a
        im[k], im[half - k] = even_im[k] + b, b - even_im[k]
    return re, im


def real_dft_transposed(re, im):
    half = len(re) - 1
    if half == 0:
        return [re[0]]
    n = 2 * half
    quarter = half // 2
    even_re, even_im = [None] * (quarter + 1), [None] * (quarter + 1)
    odd_re, odd_im = [None] * (quarter + 1), [None] * (quarter + 1)
    even_re[0], odd_re[0] = re[0] + re[half], re[0] - re[half]
    for k in range(1, quarter + 1):
        if 2 * k == half:
            even_re[k], odd_re[k] = re[k], -im[k]
            continue
        c, s = math.cos(2 * math.pi * k / n), -math.sin(2 * math.pi * k / n)
        even_re[k], even_im[k] = re[k] + re[half - k], im[k] - im[half - k]
        a, b = re[k] - re[half - k], im[k] + im[half - k]
        if 8 * k == n:
            odd_re[k], odd_im[k] = c * (a - b), c * (a + b)
        else:
            odd_re[k], odd_im[k] = c * a + s * b, c * b - s * a
    values = [None] * n
    values[0::2] = real_dft_transposed(even_re[: quarter + 1], even_im[: quarter + 1])
    values[1::2] = real_dft_transposed(odd_re[: quarter + 1], odd_im[: quarter + 1])
    return values


def flat_dft(values):
    re, im = real_dft(values)
    return re + im[1:-1]


def flat_dft_transposed(modes):
    half = len(modes) // 2
    return real_dft_transposed(modes[: half + 1], [None] + modes[half + 1 :] + [None])


def split_product(field, weights):
    width = field.shape[1]
    high = field.astype(jnp.bfloat16)
    low = (field - high.astype(jnp.float32)).astype(jnp.bfloat16)
    both = jnp.dot(
        jnp.concatenate([high, low], axis=1), weights, preferred_element_type=jnp.float32
    )
    return both[:, :width] + both[:, width:]


def kernel(
    tn, pn, t_hbm, psi_ref, weights_ref, table_ref, occupied_ref, retained_ref, out_ref,
    planes, spec, part, pair_buf, rs_buf, t_buf, a_buf, gram_ref, g_buf, inv_ref,
    load_sem, pair_send, pair_recv, rs_send, rs_recv, t_send, t_recv, a_send, a_recv, g_send, g_recv,
):
    t, p = lax.axis_index("tgt"), lax.axis_index("ptr")
    length, rows, cells = planes.shape
    lanes = psi_ref.shape[2]
    groups = lanes // length
    slab = length // pn
    all_cells = length * cells
    total_rows = tn * rows
    width = inv_ref.shape[1]
    me = t * pn + p
    devices = tn * pn
    chips = pn // 2
    chip, core = p // 2, lax.rem(p, 2)
    partner = p + 1 - 2 * core

    loads = [
        pltpu.make_async_copy(t_hbm.at[a], planes.at[:, a, :], load_sem.at[a]) for a in range(rows)
    ]
    for load in loads:
        load.start()

    barrier = pltpu.get_barrier_semaphore()

    @pl.loop(1, devices)
    def greet(d):
        other = lax.rem(me + d, devices)
        pl.semaphore_signal(
            barrier, inc=1, device_id=(other // pn, lax.rem(other, pn)), device_id_type=MESH
        )

    pl.semaphore_wait(barrier, devices - 1)
    for load in loads:
        load.wait()

    def pair_copy(q, r):
        return pltpu.make_async_remote_copy(
            src_ref=part.at[q * slab + r], dst_ref=pair_buf.at[q // 2, r],
            send_sem=pair_send.at[q // 2, r], recv_sem=pair_recv.at[q // 2, r],
            device_id=(t, partner), device_id_type=MESH,
        )

    def rs_copy(c, slot, r):
        q = 2 * c + core
        return pltpu.make_async_remote_copy(
            src_ref=part.at[q * slab + r], dst_ref=rs_buf.at[slot, r],
            send_sem=rs_send.at[c, r], recv_sem=rs_recv.at[slot, r],
            device_id=(t, q), device_id_type=MESH,
        )

    def t_copy(s, side):
        return pltpu.make_async_remote_copy(
            src_ref=t_buf.at[s], dst_ref=t_buf.at[s],
            send_sem=t_send.at[(side + 1) // 2, s], recv_sem=t_recv.at[s],
            device_id=(t + side, p), device_id_type=MESH,
        )

    def a_copy(s, side, r):
        return pltpu.make_async_remote_copy(
            src_ref=a_buf.at[s, r], dst_ref=a_buf.at[s, r],
            send_sem=a_send.at[(side + 1) // 2, s, r], recv_sem=a_recv.at[s, r],
            device_id=(t + side, p), device_id_type=MESH,
        )

    def relay(copy, hop, *at):
        for side in (-1, 1):
            s = t - side * (hop - 1)
            held = (s >= 0) & (s < tn)
            if hop > 1:

                @pl.when(held)
                def arrived():
                    copy(s, side, *at).wait_recv()

            if hop < tn:

                @pl.when(held & (t + side >= 0) & (t + side < tn))
                def onward():
                    copy(s, side, *at).start()

    def relayed(copy, *at):
        for side in (-1, 1):
            for hop in range(1, tn):
                s = t - side * (hop - 1)

                @pl.when((s >= 0) & (s < tn) & (t + side >= 0) & (t + side < tn))
                def sent():
                    copy(s, side, *at).wait_send()

    def g_copy(other, slot):
        return pltpu.make_async_remote_copy(
            src_ref=g_buf.at[me], dst_ref=g_buf.at[slot],
            send_sem=g_send.at[other], recv_sem=g_recv.at[slot],
            device_id=(other // pn, lax.rem(other, pn)), device_id_type=MESH,
        )

    t_buf[t] = planes[pl.ds(p * slab, slab)]
    relay(t_copy, 1)

    group_of = lax.broadcasted_iota(jnp.int32, (rows, lanes), 1) // length
    at_group = [group_of == g for g in range(groups)]
    per_block = groups // occupied_ref.shape[0]
    occ = 0.25 + 0.75 * occupied_ref[0].astype(jnp.float32) * jnp.ones((rows, lanes), jnp.float32)
    for i in range(1, occupied_ref.shape[0]):
        level = 0.25 + 0.75 * occupied_ref[i].astype(jnp.float32)
        occ = jnp.where(group_of >= i * per_block, level, occ)

    def pick(options):
        chosen = options[0]
        for g in range(1, groups):
            chosen = jnp.where(at_group[g], options[g], chosen)
        return chosen

    def rolled(value, steps):
        steps = steps % groups
        return value if steps == 0 else pltpu.roll(value, steps * length, 1)

    plane_rows = length * rows

    @pl.loop(0, length // FORWARD)
    def forward(i):
        density = []
        for j in range(FORWARD):
            x = i * FORWARD + j
            for q in range(length // groups):
                v = planes[x, :, q * lanes : (q + 1) * lanes]
                turned = [rolled(v, s) for s in range(groups)]
                for g in range(groups):
                    y = q * groups + g
                    spread = pick([turned[(h - g) % groups] for h in range(groups)])
                    density.append(spread * psi_ref[x, y : y + 1, :])
        waves = split_product(jnp.concatenate(density, axis=0), weights_ref[...])
        for j in range(FORWARD):
            wave = waves[j * plane_rows : (j + 1) * plane_rows]
            modes = flat_dft([wave[y * rows : (y + 1) * rows] for y in range(length)])
            for m in range(length):
                spec[i * FORWARD + j, m] = modes[m]

    relay(t_copy, 2)

    @pl.loop(0, length)
    def middle(m):
        modes = flat_dft([spec[x, m] for x in range(length)])
        half = length // 2
        scaled = []
        for i in range(length):
            k = i if i <= half else i - half
            scaled.append(modes[i] * table_ref[m, k : k + 1, :])
        values = flat_dft_transposed(scaled)
        for x in range(length):
            spec[x, m] = values[x]

    gram_ref[...] = jnp.zeros_like(gram_ref)
    relay(t_copy, 3)

    def relay_step(e):
        for hop in range(2, tn + 1):
            r = e - hop + 1
            if isinstance(e, int):
                if 0 <= r < slab:
                    relay(a_copy, hop, r)
            else:

                @pl.when(r >= 0)
                def earlier_round():
                    relay(a_copy, hop, r)

    def reduce_round(r):
        own = part[p * slab + r] + pair_buf[chip, r]
        for d in range(1, chips):
            c = lax.rem(chip + d, chips)
            rs_copy(c, c, r).wait_recv()
            own = own + rs_buf[c, r]
        a_buf[t, r] = own
        relay(a_copy, 1, r)
        relay_step(r)
        every = jnp.concatenate([t_buf[s, r] for s in range(tn)], axis=0)
        gram_ref[...] += lax.dot_general(
            own, every, (((1,), (1,)), ((), ())),
            precision=HIGHEST, preferred_element_type=jnp.float32,
        )

    @pl.loop(0, slab)
    def rounds(r):
        @pl.loop(0, pn // BACKWARD)
        def backward(i):
            away = i < chips // BACKWARD
            first = lax.rem(i * BACKWARD, chips)
            side = jnp.where(away, 1 - core, core)
            owners = [
                2 * lax.rem(chip + 1 + first + j, chips) + side for j in range(BACKWARD)
            ]
            values = []
            for q in owners:
                values += flat_dft_transposed([spec[q * slab + r, m] for m in range(length)])
            potentials = split_product(jnp.concatenate(values, axis=0), weights_ref[...])
            for j, owner in enumerate(owners):
                x = owner * slab + r
                potential = potentials[j * plane_rows : (j + 1) * plane_rows]
                for q in range(length // groups):
                    terms = []
                    for g in range(groups):
                        y = q * groups + g
                        terms.append(potential[y * rows : (y + 1) * rows] * psi_ref[x, y : y + 1, :])
                    total = None
                    for s in range(groups):
                        chosen = pick([terms[(h - s) % groups] for h in range(groups)])
                        moved = rolled(chosen * occ, -s)
                        total = moved if total is None else total + moved
                    part[x, :, q * lanes : (q + 1) * lanes] = total

            @pl.when(away)
            def to_partner():
                for owner in owners:
                    pair_copy(owner, r).start()

            @pl.when(jnp.logical_not(away))
            def to_owners():
                for j, owner in enumerate(owners):
                    pair_copy(owner, r).wait_recv()

                    @pl.when(first + j < chips - 1)
                    def send():
                        x = owner * slab + r
                        part[x] = part[x] + pair_buf[owner // 2, r]
                        rs_copy(owner // 2, chip, r).start()

        @pl.when(r == 0)
        def targets_in():
            for hop in range(4, tn + 1):
                relay(t_copy, hop)

        @pl.when(r > 0)
        def earlier():
            reduce_round(r - 1)

    reduce_round(slab - 1)

    gram = gram_ref[...] * (1.0 / all_cells)
    fold = 128 // total_rows
    short = rows // fold
    g_buf[me] = jnp.concatenate([gram[i * short : (i + 1) * short] for i in range(fold)], axis=1)

    @pl.loop(1, devices)
    def spread_gram(d):
        g_copy(lax.rem(me + d, devices), me).start()

    relay_step(slab)

    @pl.loop(1, devices)
    def collect(d):
        other = lax.rem(me + d, devices)
        g_copy(other, other).wait_recv()

    relay_step(slab + 1)
    blocks = []
    for s in range(tn):
        block = g_buf[s * pn]
        for q in range(1, pn):
            block = block + g_buf[s * pn + q]
        blocks += [block[:, i * total_rows : (i + 1) * total_rows] for i in range(fold)]
    square = jnp.concatenate(blocks, axis=0)
    square = jnp.concatenate(
        [square, jnp.zeros((total_rows, width - total_rows), jnp.float32)], axis=1
    )
    padded = jnp.concatenate([square, jnp.zeros((width - total_rows, width), jnp.float32)], axis=0)
    symmetric = 0.5 * (square + jnp.transpose(padded)[:total_rows])
    row_of = lax.broadcasted_iota(jnp.int32, (total_rows, width), 0)
    lane_of = lax.broadcasted_iota(jnp.int32, (total_rows, width), 1)
    work = jnp.where(lane_of == row_of + total_rows, 1.0, symmetric)
    for k in range(total_rows - 1):
        row = work[k : k + 1, :]
        scaled = row / work[k : k + 1, k : k + 1]
        column = jnp.where(row_of > k, work[:, k : k + 1], 0.0)
        work = work - column * scaled
    pivots = jnp.sum(jnp.where(lane_of == row_of, work, 0.0), axis=1, keepdims=True)
    keeping = (row_of < retained_ref[0]).astype(jnp.float32)
    inv_ref[...] = work * (1.0 / jnp.sqrt(pivots)) * keeping
    mine = inv_ref[pl.ds(pl.multiple_of(t * rows, rows), rows), :][:, total_rows : 2 * total_rows]
    for e in range(slab + 2, slab + tn):
        relay_step(e)
    for x in range(slab):
        every = jnp.concatenate([a_buf[s, x] for s in range(tn)], axis=0)
        out_ref[:, x, :] = jnp.dot(
            mine, every, precision=HIGHEST, preferred_element_type=jnp.float32
        )

    relayed(t_copy)
    for r in range(slab):
        for c in range(chips):
            pair_copy(2 * c + 1 - core, r).wait_send()
        for d in range(1, chips):
            rs_copy(lax.rem(chip + d, chips), chip, r).wait_send()
        relayed(a_copy, r)

    @pl.loop(1, devices)
    def drain(d):
        g_copy(lax.rem(me + d, devices), me).wait_send()


def constants(length, groups):
    i = np.arange(length)
    phase = 2.0 * np.pi / length * (i[:, None] * i[None, :] % length)
    cas = np.kron(np.eye(groups), np.cos(phase) + np.sin(phase)).astype(np.float32)
    high = cas.astype(jnp.bfloat16)
    low = (cas - high.astype(np.float32)).astype(jnp.bfloat16)
    weights = np.concatenate([np.concatenate([high, low], 1)] * 2, 0)
    signed = np.where(i < length // 2, i, i - length)
    half = length // 2
    k = np.arange(half + 1)
    wave = (2.0 * np.pi / length) ** 2
    total = wave * ((k**2)[:, None, None] + (k**2)[None, :, None] + (signed**2)[None, None, :])
    coulomb = np.where(total > 0, 4 * np.pi / np.where(total > 0, total, 1.0), 0.0)
    fold = np.where((k == 0) | (k == half), 1.0, 2.0)
    coulomb = coulomb * fold[:, None, None] * fold[None, :, None] / length**3
    order = np.concatenate([np.arange(half + 1), np.arange(1, half)])
    table = np.tile(coulomb[order], (1, 1, groups)).astype(np.float32)
    return weights, table


def shards(tn, pn, targets, partners, occupied, retained):
    rows, length, cells = targets.shape
    lanes = partners.shape[2]
    groups = lanes // length
    slab = length // pn
    weights, table = constants(length, groups)
    total_rows = tn * rows
    width = -(-2 * total_rows // 128) * 128
    vmem = pl.BlockSpec(memory_space=pltpu.VMEM)
    smem = pl.BlockSpec(memory_space=pltpu.SMEM)
    dma = pltpu.SemaphoreType.DMA
    planes = pltpu.VMEM((length, rows, cells), jnp.float32)
    block = pltpu.VMEM((tn, slab, rows, cells), jnp.float32)
    return pl.pallas_call(
        functools.partial(kernel, tn, pn),
        out_shape=jax.ShapeDtypeStruct((rows, slab, cells), jnp.float32),
        in_specs=[pl.BlockSpec(memory_space=pl.ANY), vmem, vmem, vmem, smem, smem],
        out_specs=vmem,
        scratch_shapes=[
            planes,
            pltpu.VMEM((length, length, rows, lanes), jnp.float32),
            planes,
            pltpu.VMEM((pn // 2, slab, rows, cells), jnp.float32),
            pltpu.VMEM((pn // 2, slab, rows, cells), jnp.float32),
            block,
            block,
            pltpu.VMEM((rows, total_rows), jnp.float32),
            pltpu.VMEM((tn * pn, rows * total_rows // 128, 128), jnp.float32),
            pltpu.VMEM((total_rows, width), jnp.float32),
            dma((rows,)), dma((pn // 2, slab)), dma((pn // 2, slab)), dma((pn // 2, slab)),
            dma((pn // 2, slab)), dma((2, tn)), dma((tn,)), dma((2, tn, slab)), dma((tn, slab)), dma((tn * pn,)), dma((tn * pn,)),
        ],
        compiler_params=pltpu.CompilerParams(collective_id=0, has_side_effects=True),
        name="exchange",
    )(targets, partners, jnp.asarray(weights), jnp.asarray(table), occupied, retained)


def solution(mesh):
    return jax.shard_map(
        functools.partial(shards, mesh.shape["tgt"], mesh.shape["ptr"]),
        mesh=mesh,
        in_specs=(P("tgt", None, None), P(None, None, "ptr"), P("ptr"), P()),
        out_specs=P("tgt", "ptr", None),
        check_vma=False,
    )
```

```python
import functools
import math

import jax
import jax.numpy as jnp
import numpy as np
from jax import lax
from jax.experimental import pallas as pl
from jax.experimental.pallas import tpu as pltpu
from jax.sharding import PartitionSpec as P

HIGHEST = lax.Precision.HIGHEST
MESH = pl.DeviceIdType.MESH
FORWARD = 4
BACKWARD = 4


def real_dft(values):
    n = len(values)
    if n == 1:
        return [values[0]], [None]
    even_re, even_im = real_dft(values[0::2])
    odd_re, odd_im = real_dft(values[1::2])
    half = n // 2
    re, im = [None] * (half + 1), [None] * (half + 1)
    re[0], re[half] = even_re[0] + odd_re[0], even_re[0] - odd_re[0]
    for k in range(1, half // 2 + 1):
        if 2 * k == half:
            re[k], im[k] = even_re[k], -odd_re[k]
            continue
        c, s = math.cos(2 * math.pi * k / n), -math.sin(2 * math.pi * k / n)
        if 8 * k == n:
            a = c * (odd_re[k] + odd_im[k]) if odd_im[k] is not None else c * odd_re[k]
            b = c * (odd_im[k] - odd_re[k]) if odd_im[k] is not None else -c * odd_re[k]
        else:
            a = c * odd_re[k] - s * odd_im[k]
            b = s * odd_re[k] + c * odd_im[k]
        re[k], re[half - k] = even_re[k] + a, even_re[k] - a
        im[k], im[half - k] = even_im[k] + b, b - even_im[k]
    return re, im


def real_dft_transposed(re, im):
    half = len(re) - 1
    if half == 0:
        return [re[0]]
    n = 2 * half
    quarter = half // 2
    even_re, even_im = [None] * (quarter + 1), [None] * (quarter + 1)
    odd_re, odd_im = [None] * (quarter + 1), [None] * (quarter + 1)
    even_re[0], odd_re[0] = re[0] + re[half], re[0] - re[half]
    for k in range(1, quarter + 1):
        if 2 * k == half:
            even_re[k], odd_re[k] = re[k], -im[k]
            continue
        c, s = math.cos(2 * math.pi * k / n), -math.sin(2 * math.pi * k / n)
        even_re[k], even_im[k] = re[k] + re[half - k], im[k] - im[half - k]
        a, b = re[k] - re[half - k], im[k] + im[half - k]
        if 8 * k == n:
            odd_re[k], odd_im[k] = c * (a - b), c * (a + b)
        else:
            odd_re[k], odd_im[k] = c * a + s * b, c * b - s * a
    values = [None] * n
    values[0::2] = real_dft_transposed(even_re[: quarter + 1], even_im[: quarter + 1])
    values[1::2] = real_dft_transposed(odd_re[: quarter + 1], odd_im[: quarter + 1])
    return values


def flat_dft(values):
    re, im = real_dft(values)
    return re + im[1:-1]


def flat_dft_transposed(modes):
    half = len(modes) // 2
    return real_dft_transposed(modes[: half + 1], [None] + modes[half + 1 :] + [None])


def split_product(field, weights):
    width = field.shape[1]
    high = field.astype(jnp.bfloat16)
    low = (field - high.astype(jnp.float32)).astype(jnp.bfloat16)
    both = jnp.dot(
        jnp.concatenate([high, low], axis=1), weights, preferred_element_type=jnp.float32
    )
    return both[:, :width] + both[:, width:]


def kernel(
    tn, pn, t_hbm, psi_ref, weights_ref, table_ref, occupied_ref, retained_ref, out_ref,
    planes, spec, part, pair_buf, rs_buf, t_buf, a_buf, gram_ref, g_buf, inv_ref,
    load_sem, pair_send, pair_recv, rs_send, rs_recv, t_send, t_recv, a_send, a_recv, g_send, g_recv,
):
    t, p = lax.axis_index("tgt"), lax.axis_index("ptr")
    length, rows, cells = planes.shape
    lanes = psi_ref.shape[2]
    groups = lanes // length
    slab = length // pn
    all_cells = length * cells
    total_rows = tn * rows
    width = inv_ref.shape[1]
    me = t * pn + p
    devices = tn * pn
    chips = pn // 2
    chip, core = p // 2, lax.rem(p, 2)
    partner = p + 1 - 2 * core

    loads = [
        pltpu.make_async_copy(t_hbm.at[a], planes.at[:, a, :], load_sem.at[a]) for a in range(rows)
    ]
    for load in loads:
        load.start()

    barrier = pltpu.get_barrier_semaphore()

    @pl.loop(1, devices)
    def greet(d):
        other = lax.rem(me + d, devices)
        pl.semaphore_signal(
            barrier, inc=1, device_id=(other // pn, lax.rem(other, pn)), device_id_type=MESH
        )

    pl.semaphore_wait(barrier, devices - 1)
    for load in loads:
        load.wait()

    def pair_copy(q, r):
        return pltpu.make_async_remote_copy(
            src_ref=part.at[q * slab + r], dst_ref=pair_buf.at[q // 2, r],
            send_sem=pair_send.at[q // 2, r], recv_sem=pair_recv.at[q // 2, r],
            device_id=(t, partner), device_id_type=MESH,
        )

    def rs_copy(c, slot, r):
        q = 2 * c + core
        return pltpu.make_async_remote_copy(
            src_ref=part.at[q * slab + r], dst_ref=rs_buf.at[slot, r],
            send_sem=rs_send.at[c, r], recv_sem=rs_recv.at[slot, r],
            device_id=(t, q), device_id_type=MESH,
        )

    def t_copy(s, side, h):
        piece = pl.ds(h * (slab // 2), slab // 2)
        return pltpu.make_async_remote_copy(
            src_ref=t_buf.at[s, piece], dst_ref=t_buf.at[s, piece],
            send_sem=t_send.at[(side + 1) // 2, s, h], recv_sem=t_recv.at[s, h],
            device_id=(t + side, p), device_id_type=MESH,
        )

    def a_copy(s, side, r):
        return pltpu.make_async_remote_copy(
            src_ref=a_buf.at[s, r], dst_ref=a_buf.at[s, r],
            send_sem=a_send.at[(side + 1) // 2, s, r], recv_sem=a_recv.at[s, r],
            device_id=(t + side, p), device_id_type=MESH,
        )

    def relay(copy, hop, *at):
        for side in (-1, 1):
            s = t - side * (hop - 1)
            held = (s >= 0) & (s < tn)
            if hop > 1:

                @pl.when(held)
                def arrived():
                    copy(s, side, *at).wait_recv()

            if hop < tn:

                @pl.when(held & (t + side >= 0) & (t + side < tn))
                def onward():
                    copy(s, side, *at).start()

    def relayed(copy, *at):
        for side in (-1, 1):
            for hop in range(1, tn):
                s = t - side * (hop - 1)

                @pl.when((s >= 0) & (s < tn) & (t + side >= 0) & (t + side < tn))
                def sent():
                    copy(s, side, *at).wait_send()

    def g_copy(other, slot):
        return pltpu.make_async_remote_copy(
            src_ref=g_buf.at[me], dst_ref=g_buf.at[slot],
            send_sem=g_send.at[other], recv_sem=g_recv.at[slot],
            device_id=(other // pn, lax.rem(other, pn)), device_id_type=MESH,
        )

    t_buf[t] = planes[pl.ds(p * slab, slab)]
    relay(t_copy, 1, 0)
    relay(t_copy, 1, 1)

    group_of = lax.broadcasted_iota(jnp.int32, (rows, lanes), 1) // length
    at_group = [group_of == g for g in range(groups)]
    per_block = groups // occupied_ref.shape[0]
    occ = 0.25 + 0.75 * occupied_ref[0].astype(jnp.float32) * jnp.ones((rows, lanes), jnp.float32)
    for i in range(1, occupied_ref.shape[0]):
        level = 0.25 + 0.75 * occupied_ref[i].astype(jnp.float32)
        occ = jnp.where(group_of >= i * per_block, level, occ)

    def pick(options):
        chosen = options[0]
        for g in range(1, groups):
            chosen = jnp.where(at_group[g], options[g], chosen)
        return chosen

    def rolled(value, steps):
        steps = steps % groups
        return value if steps == 0 else pltpu.roll(value, steps * length, 1)

    plane_rows = length * rows

    @pl.loop(0, length // FORWARD)
    def forward(i):
        @pl.when(i == 3 * length // (4 * FORWARD))
        def second_hop():
            relay(t_copy, 2, 0)

        density = []
        for j in range(FORWARD):
            x = i * FORWARD + j
            for q in range(length // groups):
                v = planes[x, :, q * lanes : (q + 1) * lanes]
                turned = [rolled(v, s) for s in range(groups)]
                for g in range(groups):
                    y = q * groups + g
                    spread = pick([turned[(h - g) % groups] for h in range(groups)])
                    density.append(spread * psi_ref[x, y : y + 1, :])
        waves = split_product(jnp.concatenate(density, axis=0), weights_ref[...])
        for j in range(FORWARD):
            wave = waves[j * plane_rows : (j + 1) * plane_rows]
            modes = flat_dft([wave[y * rows : (y + 1) * rows] for y in range(length)])
            for m in range(length):
                spec[i * FORWARD + j, m] = modes[m]

    relay(t_copy, 2, 1)

    @pl.loop(0, length)
    def middle(m):
        @pl.when(m == length // 2)
        def third_hop():
            relay(t_copy, 3, 0)

        modes = flat_dft([spec[x, m] for x in range(length)])
        half = length // 2
        scaled = []
        for i in range(length):
            k = i if i <= half else i - half
            scaled.append(modes[i] * table_ref[m, k : k + 1, :])
        values = flat_dft_transposed(scaled)
        for x in range(length):
            spec[x, m] = values[x]

    gram_ref[...] = jnp.zeros_like(gram_ref)
    relay(t_copy, 3, 1)

    def relay_step(e):
        for hop in range(2, tn + 1):
            r = e - hop + 1
            if isinstance(e, int):
                if 0 <= r < slab:
                    relay(a_copy, hop, r)
            else:

                @pl.when(r >= 0)
                def earlier_round():
                    relay(a_copy, hop, r)

    def reduce_round(r):
        own = part[p * slab + r] + pair_buf[chip, r]
        for d in range(1, chips):
            c = lax.rem(chip + d, chips)
            rs_copy(c, c, r).wait_recv()
            own = own + rs_buf[c, r]
        a_buf[t, r] = own
        relay(a_copy, 1, r)
        relay_step(r)
        every = jnp.concatenate([t_buf[s, r] for s in range(tn)], axis=0)
        gram_ref[...] += lax.dot_general(
            own, every, (((1,), (1,)), ((), ())),
            precision=HIGHEST, preferred_element_type=jnp.float32,
        )

    @pl.loop(0, slab)
    def rounds(r):
        @pl.loop(0, pn // BACKWARD)
        def backward(i):
            away = i < chips // BACKWARD
            first = lax.rem(i * BACKWARD, chips)
            side = jnp.where(away, 1 - core, core)
            owners = [
                2 * lax.rem(chip + 1 + first + j, chips) + side for j in range(BACKWARD)
            ]
            values = []
            for q in owners:
                values += flat_dft_transposed([spec[q * slab + r, m] for m in range(length)])
            potentials = split_product(jnp.concatenate(values, axis=0), weights_ref[...])
            for j, owner in enumerate(owners):
                x = owner * slab + r
                potential = potentials[j * plane_rows : (j + 1) * plane_rows]
                for q in range(length // groups):
                    terms = []
                    for g in range(groups):
                        y = q * groups + g
                        terms.append(potential[y * rows : (y + 1) * rows] * psi_ref[x, y : y + 1, :])
                    total = None
                    for s in range(groups):
                        chosen = pick([terms[(h - s) % groups] for h in range(groups)])
                        moved = rolled(chosen * occ, -s)
                        total = moved if total is None else total + moved
                    part[x, :, q * lanes : (q + 1) * lanes] = total

            @pl.when(away)
            def to_partner():
                for owner in owners:
                    pair_copy(owner, r).start()

            @pl.when(jnp.logical_not(away))
            def to_owners():
                for j, owner in enumerate(owners):
                    pair_copy(owner, r).wait_recv()

                    @pl.when(first + j < chips - 1)
                    def send():
                        x = owner * slab + r
                        part[x] = part[x] + pair_buf[owner // 2, r]
                        rs_copy(owner // 2, chip, r).start()

        @pl.when(r == 1)
        def targets_in():
            for hop in range(4, tn + 1):
                relay(t_copy, hop, 0)
                relay(t_copy, hop, 1)

        @pl.when(r > 0)
        def earlier():
            reduce_round(r - 1)

    reduce_round(slab - 1)

    gram = gram_ref[...] * (1.0 / all_cells)
    fold = 128 // total_rows
    short = rows // fold
    g_buf[me] = jnp.concatenate([gram[i * short : (i + 1) * short] for i in range(fold)], axis=1)

    @pl.loop(1, devices)
    def spread_gram(d):
        g_copy(lax.rem(me + d, devices), me).start()

    relay_step(slab)

    @pl.loop(1, devices)
    def collect(d):
        other = lax.rem(me + d, devices)
        g_copy(other, other).wait_recv()

    relay_step(slab + 1)
    blocks = []
    for s in range(tn):
        block = g_buf[s * pn]
        for q in range(1, pn):
            block = block + g_buf[s * pn + q]
        blocks += [block[:, i * total_rows : (i + 1) * total_rows] for i in range(fold)]
    square = jnp.concatenate(blocks, axis=0)
    square = jnp.concatenate(
        [square, jnp.zeros((total_rows, width - total_rows), jnp.float32)], axis=1
    )
    padded = jnp.concatenate([square, jnp.zeros((width - total_rows, width), jnp.float32)], axis=0)
    symmetric = 0.5 * (square + jnp.transpose(padded)[:total_rows])
    row_of = lax.broadcasted_iota(jnp.int32, (total_rows, width), 0)
    lane_of = lax.broadcasted_iota(jnp.int32, (total_rows, width), 1)
    work = jnp.where(lane_of == row_of + total_rows, 1.0, symmetric)
    for k in range(total_rows - 1):
        row = work[k : k + 1, :]
        scaled = row / work[k : k + 1, k : k + 1]
        column = jnp.where(row_of > k, work[:, k : k + 1], 0.0)
        work = work - column * scaled
    pivots = jnp.sum(jnp.where(lane_of == row_of, work, 0.0), axis=1, keepdims=True)
    keeping = (row_of < retained_ref[0]).astype(jnp.float32)
    inv_ref[...] = work * (1.0 / jnp.sqrt(pivots)) * keeping
    mine = inv_ref[pl.ds(pl.multiple_of(t * rows, rows), rows), :][:, total_rows : 2 * total_rows]
    for e in range(slab + 2, slab + tn):
        relay_step(e)
    for x in range(slab):
        every = jnp.concatenate([a_buf[s, x] for s in range(tn)], axis=0)
        out_ref[:, x, :] = jnp.dot(
            mine, every, precision=HIGHEST, preferred_element_type=jnp.float32
        )

    relayed(t_copy, 0)
    relayed(t_copy, 1)
    for r in range(slab):
        for c in range(chips):
            pair_copy(2 * c + 1 - core, r).wait_send()
        for d in range(1, chips):
            rs_copy(lax.rem(chip + d, chips), chip, r).wait_send()
        relayed(a_copy, r)

    @pl.loop(1, devices)
    def drain(d):
        g_copy(lax.rem(me + d, devices), me).wait_send()


def constants(length, groups):
    i = np.arange(length)
    phase = 2.0 * np.pi / length * (i[:, None] * i[None, :] % length)
    cas = np.kron(np.eye(groups), np.cos(phase) + np.sin(phase)).astype(np.float32)
    high = cas.astype(jnp.bfloat16)
    low = (cas - high.astype(np.float32)).astype(jnp.bfloat16)
    weights = np.concatenate([np.concatenate([high, low], 1)] * 2, 0)
    signed = np.where(i < length // 2, i, i - length)
    half = length // 2
    k = np.arange(half + 1)
    wave = (2.0 * np.pi / length) ** 2
    total = wave * ((k**2)[:, None, None] + (k**2)[None, :, None] + (signed**2)[None, None, :])
    coulomb = np.where(total > 0, 4 * np.pi / np.where(total > 0, total, 1.0), 0.0)
    fold = np.where((k == 0) | (k == half), 1.0, 2.0)
    coulomb = coulomb * fold[:, None, None] * fold[None, :, None] / length**3
    order = np.concatenate([np.arange(half + 1), np.arange(1, half)])
    table = np.tile(coulomb[order], (1, 1, groups)).astype(np.float32)
    return weights, table


def shards(tn, pn, targets, partners, occupied, retained):
    rows, length, cells = targets.shape
    lanes = partners.shape[2]
    groups = lanes // length
    slab = length // pn
    weights, table = constants(length, groups)
    total_rows = tn * rows
    width = -(-2 * total_rows // 128) * 128
    vmem = pl.BlockSpec(memory_space=pltpu.VMEM)
    smem = pl.BlockSpec(memory_space=pltpu.SMEM)
    dma = pltpu.SemaphoreType.DMA
    planes = pltpu.VMEM((length, rows, cells), jnp.float32)
    block = pltpu.VMEM((tn, slab, rows, cells), jnp.float32)
    return pl.pallas_call(
        functools.partial(kernel, tn, pn),
        out_shape=jax.ShapeDtypeStruct((rows, slab, cells), jnp.float32),
        in_specs=[pl.BlockSpec(memory_space=pl.ANY), vmem, vmem, vmem, smem, smem],
        out_specs=vmem,
        scratch_shapes=[
            planes,
            pltpu.VMEM((length, length, rows, lanes), jnp.float32),
            planes,
            pltpu.VMEM((pn // 2, slab, rows, cells), jnp.float32),
            pltpu.VMEM((pn // 2, slab, rows, cells), jnp.float32),
            block,
            block,
            pltpu.VMEM((rows, total_rows), jnp.float32),
            pltpu.VMEM((tn * pn, rows * total_rows // 128, 128), jnp.float32),
            pltpu.VMEM((total_rows, width), jnp.float32),
            dma((rows,)), dma((pn // 2, slab)), dma((pn // 2, slab)), dma((pn // 2, slab)),
            dma((pn // 2, slab)), dma((2, tn, 2)), dma((tn, 2)), dma((2, tn, slab)), dma((tn, slab)), dma((tn * pn,)), dma((tn * pn,)),
        ],
        compiler_params=pltpu.CompilerParams(collective_id=0, has_side_effects=True),
        name="exchange",
    )(targets, partners, jnp.asarray(weights), jnp.asarray(table), occupied, retained)


def solution(mesh):
    return jax.shard_map(
        functools.partial(shards, mesh.shape["tgt"], mesh.shape["ptr"]),
        mesh=mesh,
        in_specs=(P("tgt", None, None), P(None, None, "ptr"), P("ptr"), P()),
        out_specs=P("tgt", "ptr", None),
        check_vma=False,
    )
```

```python
import functools
import math

import jax
import jax.numpy as jnp
import numpy as np
from jax import lax
from jax.experimental import pallas as pl
from jax.experimental.pallas import tpu as pltpu
from jax.sharding import PartitionSpec as P

HIGHEST = lax.Precision.HIGHEST
MESH = pl.DeviceIdType.MESH
FORWARD = 4
BACKWARD = 4


def real_dft(values):
    n = len(values)
    if n == 1:
        return [values[0]], [None]
    even_re, even_im = real_dft(values[0::2])
    odd_re, odd_im = real_dft(values[1::2])
    half = n // 2
    re, im = [None] * (half + 1), [None] * (half + 1)
    re[0], re[half] = even_re[0] + odd_re[0], even_re[0] - odd_re[0]
    for k in range(1, half // 2 + 1):
        if 2 * k == half:
            re[k], im[k] = even_re[k], -odd_re[k]
            continue
        c, s = math.cos(2 * math.pi * k / n), -math.sin(2 * math.pi * k / n)
        if 8 * k == n:
            a = c * (odd_re[k] + odd_im[k]) if odd_im[k] is not None else c * odd_re[k]
            b = c * (odd_im[k] - odd_re[k]) if odd_im[k] is not None else -c * odd_re[k]
        else:
            a = c * odd_re[k] - s * odd_im[k]
            b = s * odd_re[k] + c * odd_im[k]
        re[k], re[half - k] = even_re[k] + a, even_re[k] - a
        im[k], im[half - k] = even_im[k] + b, b - even_im[k]
    return re, im


def real_dft_transposed(re, im):
    half = len(re) - 1
    if half == 0:
        return [re[0]]
    n = 2 * half
    quarter = half // 2
    even_re, even_im = [None] * (quarter + 1), [None] * (quarter + 1)
    odd_re, odd_im = [None] * (quarter + 1), [None] * (quarter + 1)
    even_re[0], odd_re[0] = re[0] + re[half], re[0] - re[half]
    for k in range(1, quarter + 1):
        if 2 * k == half:
            even_re[k], odd_re[k] = re[k], -im[k]
            continue
        c, s = math.cos(2 * math.pi * k / n), -math.sin(2 * math.pi * k / n)
        even_re[k], even_im[k] = re[k] + re[half - k], im[k] - im[half - k]
        a, b = re[k] - re[half - k], im[k] + im[half - k]
        if 8 * k == n:
            odd_re[k], odd_im[k] = c * (a - b), c * (a + b)
        else:
            odd_re[k], odd_im[k] = c * a + s * b, c * b - s * a
    values = [None] * n
    values[0::2] = real_dft_transposed(even_re[: quarter + 1], even_im[: quarter + 1])
    values[1::2] = real_dft_transposed(odd_re[: quarter + 1], odd_im[: quarter + 1])
    return values


def flat_dft(values):
    re, im = real_dft(values)
    return re + im[1:-1]


def flat_dft_transposed(modes):
    half = len(modes) // 2
    return real_dft_transposed(modes[: half + 1], [None] + modes[half + 1 :] + [None])


def split_product(field, weights):
    width = field.shape[1]
    high = field.astype(jnp.bfloat16)
    low = (field - high.astype(jnp.float32)).astype(jnp.bfloat16)
    both = jnp.dot(
        jnp.concatenate([high, low], axis=1), weights, preferred_element_type=jnp.float32
    )
    return both[:, :width] + both[:, width:]


def kernel(
    tn, pn, t_hbm, psi_ref, weights_ref, table_ref, occupied_ref, retained_ref, out_ref,
    planes, spec, part, pair_buf, rs_buf, t_buf, a_buf, gram_ref, g_buf, inv_ref,
    load_sem, pair_send, pair_recv, rs_send, rs_recv, t_send, t_recv, a_send, a_recv, g_send, g_recv,
):
    t, p = lax.axis_index("tgt"), lax.axis_index("ptr")
    length, rows, cells = planes.shape
    lanes = psi_ref.shape[2]
    groups = lanes // length
    slab = length // pn
    all_cells = length * cells
    total_rows = tn * rows
    width = inv_ref.shape[1]
    me = t * pn + p
    devices = tn * pn
    chips = pn // 2
    chip, core = p // 2, lax.rem(p, 2)
    partner = p + 1 - 2 * core

    loads = [
        pltpu.make_async_copy(t_hbm.at[a], planes.at[:, a, :], load_sem.at[a]) for a in range(rows)
    ]
    for load in loads:
        load.start()

    barrier = pltpu.get_barrier_semaphore()

    @pl.loop(1, devices)
    def greet(d):
        other = lax.rem(me + d, devices)
        pl.semaphore_signal(
            barrier, inc=1, device_id=(other // pn, lax.rem(other, pn)), device_id_type=MESH
        )

    pl.semaphore_wait(barrier, devices - 1)
    for load in loads:
        load.wait()

    def pair_copy(q, r):
        return pltpu.make_async_remote_copy(
            src_ref=part.at[q * slab + r], dst_ref=pair_buf.at[q // 2, r],
            send_sem=pair_send.at[q // 2, r], recv_sem=pair_recv.at[q // 2, r],
            device_id=(t, partner), device_id_type=MESH,
        )

    def rs_copy(c, slot, r):
        q = 2 * c + core
        return pltpu.make_async_remote_copy(
            src_ref=part.at[q * slab + r], dst_ref=rs_buf.at[slot, r],
            send_sem=rs_send.at[c, r], recv_sem=rs_recv.at[slot, r],
            device_id=(t, q), device_id_type=MESH,
        )

    def t_copy(s, side, h):
        piece = pl.ds(h * (slab // 2), slab // 2)
        return pltpu.make_async_remote_copy(
            src_ref=t_buf.at[s, piece], dst_ref=t_buf.at[s, piece],
            send_sem=t_send.at[(side + 1) // 2, s, h], recv_sem=t_recv.at[s, h],
            device_id=(t + side, p), device_id_type=MESH,
        )

    def a_copy(s, side, r):
        return pltpu.make_async_remote_copy(
            src_ref=a_buf.at[s, r], dst_ref=a_buf.at[s, r],
            send_sem=a_send.at[(side + 1) // 2, s, r], recv_sem=a_recv.at[s, r],
            device_id=(t + side, p), device_id_type=MESH,
        )

    def relay(copy, hop, *at):
        for side in (-1, 1):
            s = t - side * (hop - 1)
            held = (s >= 0) & (s < tn)
            if hop > 1:

                @pl.when(held)
                def arrived():
                    copy(s, side, *at).wait_recv()

            if hop < tn:

                @pl.when(held & (t + side >= 0) & (t + side < tn))
                def onward():
                    copy(s, side, *at).start()

    def relayed(copy, *at):
        for side in (-1, 1):
            for hop in range(1, tn):
                s = t - side * (hop - 1)

                @pl.when((s >= 0) & (s < tn) & (t + side >= 0) & (t + side < tn))
                def sent():
                    copy(s, side, *at).wait_send()

    def g_copy(other, slot):
        return pltpu.make_async_remote_copy(
            src_ref=g_buf.at[me], dst_ref=g_buf.at[slot],
            send_sem=g_send.at[other], recv_sem=g_recv.at[slot],
            device_id=(other // pn, lax.rem(other, pn)), device_id_type=MESH,
        )

    t_buf[t] = planes[pl.ds(p * slab, slab)]
    relay(t_copy, 1, 0)
    relay(t_copy, 1, 1)

    group_of = lax.broadcasted_iota(jnp.int32, (rows, lanes), 1) // length
    at_group = [group_of == g for g in range(groups)]
    per_block = groups // occupied_ref.shape[0]
    occ = 0.25 + 0.75 * occupied_ref[0].astype(jnp.float32) * jnp.ones((rows, lanes), jnp.float32)
    for i in range(1, occupied_ref.shape[0]):
        level = 0.25 + 0.75 * occupied_ref[i].astype(jnp.float32)
        occ = jnp.where(group_of >= i * per_block, level, occ)

    def pick(options):
        chosen = options[0]
        for g in range(1, groups):
            chosen = jnp.where(at_group[g], options[g], chosen)
        return chosen

    def rolled(value, steps):
        steps = steps % groups
        return value if steps == 0 else pltpu.roll(value, steps * length, 1)

    plane_rows = length * rows

    @pl.loop(0, length // FORWARD)
    def forward(i):
        @pl.when(i == 3 * length // (4 * FORWARD))
        def second_hop():
            relay(t_copy, 2, 0)

        density = []
        for j in range(FORWARD):
            x = i * FORWARD + j
            for q in range(length // groups):
                v = planes[x, :, q * lanes : (q + 1) * lanes]
                turned = [rolled(v, s) for s in range(groups)]
                for g in range(groups):
                    y = q * groups + g
                    spread = pick([turned[(h - g) % groups] for h in range(groups)])
                    density.append(spread * psi_ref[x, y : y + 1, :])
        waves = split_product(jnp.concatenate(density, axis=0), weights_ref[...])
        for j in range(FORWARD):
            wave = waves[j * plane_rows : (j + 1) * plane_rows]
            modes = flat_dft([wave[y * rows : (y + 1) * rows] for y in range(length)])
            for m in range(length):
                spec[i * FORWARD + j, m] = modes[m]

    relay(t_copy, 2, 1)

    @pl.loop(0, length)
    def middle(m):
        @pl.when(m == length // 2)
        def third_hop():
            relay(t_copy, 3, 0)

        modes = flat_dft([spec[x, m] for x in range(length)])
        half = length // 2
        scaled = []
        for i in range(length):
            k = i if i <= half else i - half
            scaled.append(modes[i] * table_ref[m, k : k + 1, :])
        values = flat_dft_transposed(scaled)
        for x in range(length):
            spec[x, m] = values[x]

    gram_ref[...] = jnp.zeros_like(gram_ref)
    relay(t_copy, 3, 1)

    def relay_step(e):
        for hop in range(2, tn + 1):
            r = e - 2 * (hop - 1)
            if isinstance(e, int):
                if 0 <= r < slab:
                    relay(a_copy, hop, r)
            else:

                @pl.when(r >= 0)
                def earlier_round():
                    relay(a_copy, hop, r)

    def reduce_round(r):
        own = part[p * slab + r] + pair_buf[chip, r]
        for d in range(1, chips):
            c = lax.rem(chip + d, chips)
            rs_copy(c, c, r).wait_recv()
            own = own + rs_buf[c, r]
        a_buf[t, r] = own
        relay(a_copy, 1, r)
        relay_step(r)

    def add_gram(r):
        every = jnp.concatenate([t_buf[s, r] for s in range(tn)], axis=0)
        gram_ref[...] += lax.dot_general(
            a_buf[t, r], every, (((1,), (1,)), ((), ())),
            precision=HIGHEST, preferred_element_type=jnp.float32,
        )

    @pl.loop(0, slab)
    def rounds(r):
        @pl.loop(0, pn // BACKWARD)
        def backward(i):
            away = i < chips // BACKWARD
            first = lax.rem(i * BACKWARD, chips)
            side = jnp.where(away, 1 - core, core)
            owners = [
                2 * lax.rem(chip + 1 + first + j, chips) + side for j in range(BACKWARD)
            ]
            values = []
            for q in owners:
                values += flat_dft_transposed([spec[q * slab + r, m] for m in range(length)])
            potentials = split_product(jnp.concatenate(values, axis=0), weights_ref[...])
            for j, owner in enumerate(owners):
                x = owner * slab + r
                potential = potentials[j * plane_rows : (j + 1) * plane_rows]
                for q in range(length // groups):
                    terms = []
                    for g in range(groups):
                        y = q * groups + g
                        terms.append(potential[y * rows : (y + 1) * rows] * psi_ref[x, y : y + 1, :])
                    total = None
                    for s in range(groups):
                        chosen = pick([terms[(h - s) % groups] for h in range(groups)])
                        moved = rolled(chosen * occ, -s)
                        total = moved if total is None else total + moved
                    part[x, :, q * lanes : (q + 1) * lanes] = total

            @pl.when(away)
            def to_partner():
                for owner in owners:
                    pair_copy(owner, r).start()

            @pl.when(jnp.logical_not(away))
            def to_owners():
                for j, owner in enumerate(owners):
                    pair_copy(owner, r).wait_recv()

                    @pl.when(first + j < chips - 1)
                    def send():
                        x = owner * slab + r
                        part[x] = part[x] + pair_buf[owner // 2, r]
                        rs_copy(owner // 2, chip, r).start()

        @pl.when(r > 1)
        def earlier():
            reduce_round(r - 2)

    for hop in range(4, tn + 1):
        relay(t_copy, hop, 0)
        relay(t_copy, hop, 1)
    for r in range(slab - 2):
        add_gram(r)
    for r in range(slab - 2, slab):
        reduce_round(r)
        add_gram(r)

    gram = gram_ref[...] * (1.0 / all_cells)
    fold = 128 // total_rows
    short = rows // fold
    g_buf[me] = jnp.concatenate([gram[i * short : (i + 1) * short] for i in range(fold)], axis=1)

    @pl.loop(1, devices)
    def spread_gram(d):
        g_copy(lax.rem(me + d, devices), me).start()

    relay_step(slab)
    relay_step(slab + 1)

    @pl.loop(1, devices)
    def collect(d):
        other = lax.rem(me + d, devices)
        g_copy(other, other).wait_recv()

    relay_step(slab + 2)
    relay_step(slab + 3)
    blocks = []
    for s in range(tn):
        block = g_buf[s * pn]
        for q in range(1, pn):
            block = block + g_buf[s * pn + q]
        blocks += [block[:, i * total_rows : (i + 1) * total_rows] for i in range(fold)]
    square = jnp.concatenate(blocks, axis=0)
    square = jnp.concatenate(
        [square, jnp.zeros((total_rows, width - total_rows), jnp.float32)], axis=1
    )
    padded = jnp.concatenate([square, jnp.zeros((width - total_rows, width), jnp.float32)], axis=0)
    symmetric = 0.5 * (square + jnp.transpose(padded)[:total_rows])
    row_of = lax.broadcasted_iota(jnp.int32, (total_rows, width), 0)
    lane_of = lax.broadcasted_iota(jnp.int32, (total_rows, width), 1)
    work = jnp.where(lane_of == row_of + total_rows, 1.0, symmetric)
    for k in range(total_rows - 1):
        row = work[k : k + 1, :]
        scaled = row / work[k : k + 1, k : k + 1]
        column = jnp.where(row_of > k, work[:, k : k + 1], 0.0)
        work = work - column * scaled
    pivots = jnp.sum(jnp.where(lane_of == row_of, work, 0.0), axis=1, keepdims=True)
    keeping = (row_of < retained_ref[0]).astype(jnp.float32)
    inv_ref[...] = work * (1.0 / jnp.sqrt(pivots)) * keeping
    mine = inv_ref[pl.ds(pl.multiple_of(t * rows, rows), rows), :][:, total_rows : 2 * total_rows]
    for e in range(slab + 4, slab + 2 * (tn - 1)):
        relay_step(e)
    for x in range(slab):
        every = jnp.concatenate([a_buf[s, x] for s in range(tn)], axis=0)
        out_ref[:, x, :] = jnp.dot(
            mine, every, precision=HIGHEST, preferred_element_type=jnp.float32
        )

    relayed(t_copy, 0)
    relayed(t_copy, 1)
    for r in range(slab):
        for c in range(chips):
            pair_copy(2 * c + 1 - core, r).wait_send()
        for d in range(1, chips):
            rs_copy(lax.rem(chip + d, chips), chip, r).wait_send()
        relayed(a_copy, r)

    @pl.loop(1, devices)
    def drain(d):
        g_copy(lax.rem(me + d, devices), me).wait_send()


def constants(length, groups):
    i = np.arange(length)
    phase = 2.0 * np.pi / length * (i[:, None] * i[None, :] % length)
    cas = np.kron(np.eye(groups), np.cos(phase) + np.sin(phase)).astype(np.float32)
    high = cas.astype(jnp.bfloat16)
    low = (cas - high.astype(np.float32)).astype(jnp.bfloat16)
    weights = np.concatenate([np.concatenate([high, low], 1)] * 2, 0)
    signed = np.where(i < length // 2, i, i - length)
    half = length // 2
    k = np.arange(half + 1)
    wave = (2.0 * np.pi / length) ** 2
    total = wave * ((k**2)[:, None, None] + (k**2)[None, :, None] + (signed**2)[None, None, :])
    coulomb = np.where(total > 0, 4 * np.pi / np.where(total > 0, total, 1.0), 0.0)
    fold = np.where((k == 0) | (k == half), 1.0, 2.0)
    coulomb = coulomb * fold[:, None, None] * fold[None, :, None] / length**3
    order = np.concatenate([np.arange(half + 1), np.arange(1, half)])
    table = np.tile(coulomb[order], (1, 1, groups)).astype(np.float32)
    return weights, table


def shards(tn, pn, targets, partners, occupied, retained):
    rows, length, cells = targets.shape
    lanes = partners.shape[2]
    groups = lanes // length
    slab = length // pn
    weights, table = constants(length, groups)
    total_rows = tn * rows
    width = -(-2 * total_rows // 128) * 128
    vmem = pl.BlockSpec(memory_space=pltpu.VMEM)
    smem = pl.BlockSpec(memory_space=pltpu.SMEM)
    dma = pltpu.SemaphoreType.DMA
    planes = pltpu.VMEM((length, rows, cells), jnp.float32)
    block = pltpu.VMEM((tn, slab, rows, cells), jnp.float32)
    return pl.pallas_call(
        functools.partial(kernel, tn, pn),
        out_shape=jax.ShapeDtypeStruct((rows, slab, cells), jnp.float32),
        in_specs=[pl.BlockSpec(memory_space=pl.ANY), vmem, vmem, vmem, smem, smem],
        out_specs=vmem,
        scratch_shapes=[
            planes,
            pltpu.VMEM((length, length, rows, lanes), jnp.float32),
            planes,
            pltpu.VMEM((pn // 2, slab, rows, cells), jnp.float32),
            pltpu.VMEM((pn // 2, slab, rows, cells), jnp.float32),
            block,
            block,
            pltpu.VMEM((rows, total_rows), jnp.float32),
            pltpu.VMEM((tn * pn, rows * total_rows // 128, 128), jnp.float32),
            pltpu.VMEM((total_rows, width), jnp.float32),
            dma((rows,)), dma((pn // 2, slab)), dma((pn // 2, slab)), dma((pn // 2, slab)),
            dma((pn // 2, slab)), dma((2, tn, 2)), dma((tn, 2)), dma((2, tn, slab)), dma((tn, slab)), dma((tn * pn,)), dma((tn * pn,)),
        ],
        compiler_params=pltpu.CompilerParams(collective_id=0, has_side_effects=True),
        name="exchange",
    )(targets, partners, jnp.asarray(weights), jnp.asarray(table), occupied, retained)


def solution(mesh):
    return jax.shard_map(
        functools.partial(shards, mesh.shape["tgt"], mesh.shape["ptr"]),
        mesh=mesh,
        in_specs=(P("tgt", None, None), P(None, None, "ptr"), P("ptr"), P()),
        out_specs=P("tgt", "ptr", None),
        check_vma=False,
    )
```
